32 devices in a mesh: row: 8 (over y, x, core), col: 4 (over z).
Axes of the slice: x: 2, y: 2, z: 4, core: 2. Of those that a mesh axis runs over, the one named last changes fastest.
Arguments:
- inverse_blocks: float32 [4096, 4096], P('row', 'col'), may hold values from -0.09375 to 0.09375
- panel: bfloat16 [4096, 4096], P('row', 'col'), may hold values from -1.5 to 1.5
- diag_inverse: float32 [512, 4096], P('row', 'col'), may hold values from -6 to 6
- members: int32 [8, 8], replicated, may hold values from 0 to 7, each once within a row
- counts: int32 [8], replicated, may hold values from 1 to 8, as said below
Outputs:
- offdiag: float32 [4096, 4096], P('row', 'col')
- new_diag: float32 [512, 4096], P('row', 'col')
The draws below stay inside these ranges and needn't reach their ends.
Inputs may be any that keep to these rules, and one draw needn't show every extreme that they name: Each row of members names every ancestor once. `counts`: some supernode lists all 8 ancestors and some lists one.
All inputs are finite; a program needn't handle non-finite values.
Results may differ from the reference program's by a relative error of at most 0.0003.
Values may be sent and summed in bfloat16 or wider, within the bound.
A program may use at most 128 MiB of HBM per device.

```python
import jax
import jax.numpy as jnp
from jax import lax

B = 512
NA = 8
G = 8


def draw_counts(key, part):
    first_key, second_key = jax.random.split(jax.random.fold_in(key, 7))
    drawn_counts = jax.random.randint(first_key, (G,), 1, NA + 1)
    spot_index = jax.random.randint(second_key, (), 0, G)
    position = jnp.arange(G, dtype=jnp.int32)
    drawn_counts = jnp.where(position == spot_index, NA, drawn_counts)
    drawn_counts = jnp.where(position == (spot_index + 1) % G, 1, drawn_counts)
    return drawn_counts.astype(jnp.int32)


def level_of(key, shape, cuts, smallest, largest):
    def one(dim, blocks):
        draws = jax.random.uniform(jax.random.fold_in(jax.random.fold_in(key, 6), dim), (blocks,), jnp.float32, smallest / len(cuts), largest / len(cuts))
        return jnp.repeat(jnp.exp(draws), shape[dim] // blocks).reshape((-1,) + (1,) * (len(shape) - dim - 1))

    loudness = one(*cuts[0])
    for cut in cuts[1:]:
        loudness = loudness * one(*cut)
    return loudness


def bell_draw(rng, extent, width, bound, cuts=(), kind=jnp.bfloat16):
    array = jax.random.normal(rng, extent, jnp.float32) * width
    if len(cuts) > 0:
        array = level_of(rng, extent, cuts, -0.22, 0.18) * array
    return jnp.clip(array, min=-bound, max=bound).astype(kind)


def setup_inputs(seed: int = 0) -> dict:
    key_of = jax.random.split(jax.random.key(seed), 6)
    return {
        "inverse_blocks": bell_draw(key_of[0], (NA * B, NA * B), (NA * B) ** -0.5, 0.09375, ((0, 8), (1, 4)), jnp.float32),
        "panel": bell_draw(key_of[1], (NA * B, G * B), 0.25, 1.5, ((0, 8), (1, 4))),
        "diag_inverse": bell_draw(key_of[2], (B, G * B), 1.0, 6.0, ((0, 8), (1, 4)), jnp.float32),
        "members": jax.vmap(lambda own: jax.random.permutation(own, NA))(jax.random.split(key_of[3], G)).reshape((G, NA)).astype(jnp.int32),
        "counts": draw_counts(jax.random.fold_in(key_of[5], 71), 0),
    }


def reference(inverse_blocks, panel, diag_inverse, members, counts):
    slot_index = jnp.arange(NA, dtype=jnp.int32)
    live_slot = slot_index[None, :] < counts[:, None]
    is_member = (members[:, :, None] == slot_index[None, None, :]) & live_slot[:, :, None]
    member_mask = jnp.sum(jnp.where(is_member, 1.0, 0.0).astype(jnp.float32), axis=1)
    block_mask = jnp.transpose(member_mask)[:, None, :, None]
    masked_blocks = panel.astype(jnp.float32).reshape(NA, B, G, B) * block_mask
    product = jnp.dot(inverse_blocks, masked_blocks.reshape(NA * B, G * B), precision=lax.Precision.HIGHEST)
    offdiag_blocks = -(product.reshape(NA, B, G, B) * block_mask)
    diag_terms = jnp.einsum("jikc,jikd->ckd", masked_blocks, offdiag_blocks, precision=lax.Precision.HIGHEST)
    new_diag = diag_inverse - diag_terms.reshape(B, G * B)
    return offdiag_blocks.reshape(NA * B, G * B), new_diag
```

```python
import jax
import jax.numpy as jnp
from jax import lax
from jax.sharding import PartitionSpec as P

B = 512


def quantize(block):
    peak = jnp.max(jnp.abs(block), axis=1, keepdims=True)
    live = peak > 1e-30
    safe = jnp.where(live, peak, 1.0)
    coded = jnp.round(block * (32767.0 / safe)).astype(jnp.int16)
    return jnp.where(live, coded, 0), safe * (1.0 / 32767.0)


def split_code(coded):
    wide = coded.astype(jnp.int32)
    high = (wide + 64) & -128
    return high.astype(jnp.bfloat16), (wide - high).astype(jnp.bfloat16)


def column_masks(members, counts, ancestor, first_sup, sup_count):
    local_members = lax.dynamic_slice_in_dim(members, first_sup, sup_count, 0)
    local_counts = lax.dynamic_slice_in_dim(counts, first_sup, sup_count, 0)
    slot_index = jnp.arange(members.shape[1], dtype=jnp.int32)
    live_slot = slot_index[None, :] < local_counts[:, None]
    row_mask = jnp.sum(
        jnp.where((local_members == ancestor) & live_slot, 1.0, 0.0).astype(jnp.float32), axis=1
    )
    return jnp.repeat(row_mask, B)


def body(inverse_blocks, panel, diag_inverse, members, counts):
    rows_dev, cols_dev = panel.shape
    sup_count = cols_dev // B
    depth = inverse_blocks.shape[1]
    ancestor = lax.axis_index("row") * rows_dev // B
    column_mask = column_masks(members, counts, ancestor, lax.axis_index("col") * sup_count, sup_count)
    masked = panel * column_mask.astype(jnp.bfloat16)[None, :]
    coded, scale = quantize(inverse_blocks)
    coded_all = lax.all_gather(coded, "col", axis=0, tiled=False)
    scale_all = lax.all_gather(scale, "col", axis=0, tiled=False)
    masked_all = lax.all_gather(masked, "row", axis=0, tiled=True)
    running = jnp.zeros((rows_dev, cols_dev), jnp.float32)
    for shard in range(coded_all.shape[0]):
        high, low = split_code(coded_all[shard])
        part = masked_all[shard * depth : (shard + 1) * depth]
        term = jnp.dot(high, part, preferred_element_type=jnp.float32) + jnp.dot(
            low, part, preferred_element_type=jnp.float32
        )
        running = running + scale_all[shard] * term
    offdiag = -(running * column_mask[None, :])
    off_high = lax.reduce_precision(offdiag, 8, 7)
    off_low = (offdiag - off_high).astype(jnp.bfloat16).reshape(rows_dev, sup_count, B)
    off_high = off_high.astype(jnp.bfloat16).reshape(rows_dev, sup_count, B)
    masked_blocks = masked.reshape(rows_dev, sup_count, B)
    diag_terms = jnp.einsum(
        "ikc,ikd->ckd", masked_blocks, off_high, preferred_element_type=jnp.float32
    ) + jnp.einsum("ikc,ikd->ckd", masked_blocks, off_low, preferred_element_type=jnp.float32)
    summed = lax.psum_scatter(
        diag_terms.reshape(B, sup_count * B), "row", scatter_dimension=0, tiled=True
    )
    return (offdiag, diag_inverse - summed)


def solution(mesh):
    return jax.shard_map(
        body,
        mesh=mesh,
        in_specs=(P("row", "col"), P("row", "col"), P("row", "col"), P(), P()),
        out_specs=(P("row", "col"), P("row", "col")),
        check_vma=False,
    )
```

```python
import jax
import jax.numpy as jnp
from jax import lax
from jax.experimental import pallas as pl
from jax.experimental.pallas import tpu as pltpu
from jax.sharding import PartitionSpec as P

B = 512


def quantize(block):
    peak = jnp.max(jnp.abs(block), axis=1, keepdims=True)
    live = peak > 1e-30
    safe = jnp.where(live, peak, 1.0)
    coded = jnp.round(block * (32767.0 / safe)).astype(jnp.int16)
    return jnp.where(live, coded, 0), safe * (1.0 / 32767.0)


def split_code(coded):
    wide = coded.astype(jnp.int32)
    high = (wide + 64) & -128
    return high.astype(jnp.bfloat16), (wide - high).astype(jnp.bfloat16)


def column_masks(members, counts, ancestor, first_sup, sup_count):
    local_members = lax.dynamic_slice_in_dim(members, first_sup, sup_count, 0)
    local_counts = lax.dynamic_slice_in_dim(counts, first_sup, sup_count, 0)
    slot_index = jnp.arange(members.shape[1], dtype=jnp.int32)
    live_slot = slot_index[None, :] < local_counts[:, None]
    row_mask = jnp.sum(
        jnp.where((local_members == ancestor) & live_slot, 1.0, 0.0).astype(jnp.float32), axis=1
    )
    return jnp.repeat(row_mask, B)


MESH = pl.DeviceIdType.MESH
PIECE = 128
TILE = 256


def fused_kernel(
    inv_ref, panel_ref, mask_ref, diag_ref, off_ref, new_ref,
    coded, scales, wide_scale, blocks, stacked, partial, from_twin, chip_sum, from_chips,
    a_recv, a_right, a_left, s_recv, s_right, s_left,
    p_recv, p_send, p_twin, t_recv, t_send, c_recv, c_send,
):
    n = coded.shape[0]
    rows, depth = inv_ref.shape
    cols = panel_ref.shape[1]
    pieces = rows // PIECE
    me = lax.axis_index("row")
    z = lax.axis_index("col")
    chip, core = lax.div(me, 2), lax.rem(me, 2)
    y, x = lax.div(chip, 2), lax.rem(chip, 2)
    twin = chip * 2 + (1 - core)
    others = (y * 2 + (1 - x), (1 - y) * 2 + x, (1 - y) * 2 + (1 - x))

    def far(src, dst, send, recv, row, col):
        return pltpu.make_async_remote_copy(
            src_ref=src, dst_ref=dst, send_sem=send, recv_sem=recv,
            device_id=(row, col), device_id_type=MESH,
        )

    def right_piece(c, p):
        ref = coded.at[c, pl.ds(pl.multiple_of(p * PIECE, PIECE), PIECE)]
        return far(ref, ref, a_right.at[c, p], a_recv.at[c, p], me, z + 1)

    def left_piece(c, p):
        ref = coded.at[c, pl.ds(pl.multiple_of(p * PIECE, PIECE), PIECE)]
        return far(ref, ref, a_left.at[c, p], a_recv.at[c, p], me, z - 1)

    def right_scale(c):
        return far(scales.at[c], scales.at[c], s_right.at[c], s_recv.at[c], me, z + 1)

    def left_scale(c):
        return far(scales.at[c], scales.at[c], s_left.at[c], s_recv.at[c], me, z - 1)

    def panel_to(d):
        return far(blocks.at[me], blocks.at[me], p_send.at[d], p_recv.at[me], others[d] * 2 + core, z)

    def panel_twin(d):
        r = me if d == 3 else others[d] * 2 + core
        return far(blocks.at[r], blocks.at[r], p_twin.at[d], p_recv.at[r], twin, z)

    def panel_arrived(r):
        far(blocks.at[r], blocks.at[r], p_twin.at[0], p_recv.at[r], twin, z).wait_recv()

    barrier = pltpu.get_barrier_semaphore()
    for row in [twin] + [o * 2 + core for o in others]:
        pl.semaphore_signal(barrier, inc=1, device_id=(row, z), device_id_type=MESH)

    @pl.when(z > 0)
    def _():
        pl.semaphore_signal(barrier, inc=1, device_id=(me, z - 1), device_id_type=MESH)

    @pl.when(z < n - 1)
    def _():
        pl.semaphore_signal(barrier, inc=1, device_id=(me, z + 1), device_id_type=MESH)

    block = inv_ref[...]
    peak = jnp.max(jnp.abs(block), axis=1, keepdims=True)
    live = peak > 1e-33
    safe = jnp.where(live, peak, 1.0)
    ratio = jnp.where(live, 32767.0 / safe, 0.0)
    ready = block * ratio
    ready = ready + jnp.where(ready >= 0.0, 0.5, -0.5)
    coded[z] = ready.astype(jnp.int32).astype(jnp.int16)
    step = jnp.broadcast_to(safe * (1.0 / 32767.0), (rows, 128))
    scales[z] = step.T[:8]
    blocks[me] = panel_ref[...] * mask_ref[...].astype(jnp.bfloat16)

    pl.semaphore_wait(barrier, 4 + jnp.where(z > 0, 1, 0) + jnp.where(z < n - 1, 1, 0))

    @pl.when(z < n - 1)
    def _():
        right_scale(z).start()

        @pl.loop(0, pieces)
        def _(p):
            right_piece(z, p).start()

    @pl.when(z > 0)
    def _():
        left_scale(z).start()

        @pl.loop(0, pieces)
        def _(p):
            left_piece(z, p).start()

    panel_twin(3).start()
    for d in range(3):
        panel_to(d).start()
    off_ref[...] = jnp.zeros_like(off_ref)
    partial[...] = jnp.zeros_like(partial)

    def relay(s):
        @pl.loop(0, pieces)
        def _(p):
            @pl.when(z >= s)
            def _():
                @pl.when(p == 0)
                def _():
                    right_scale(z - s).wait_recv()

                right_piece(z - s, p).wait_recv()

                @pl.when(z < n - 1)
                def _():
                    @pl.when(p == 0)
                    def _():
                        right_scale(z - s).start()

                    right_piece(z - s, p).start()

            @pl.when(z + s < n)
            def _():
                @pl.when(p == 0)
                def _():
                    left_scale(z + s).wait_recv()

                left_piece(z + s, p).wait_recv()

                @pl.when(z > 0)
                def _():
                    @pl.when(p == 0)
                    def _():
                        left_scale(z + s).start()

                    left_piece(z + s, p).start()

    def widen(c):
        eight = scales[c]
        wide_scale[...] = jnp.concatenate([eight] * 16, axis=0).T

    def accumulate(c, first, count):
        span = pl.ds(first, count)
        code = coded[c, span, :].astype(jnp.int32)
        high = (code + 64) & -128
        stacked[0:count] = high.astype(jnp.float32).astype(jnp.bfloat16)
        stacked[count : 2 * count] = (code - high).astype(jnp.float32).astype(jnp.bfloat16)
        step = wide_scale[span, :]
        step = jnp.concatenate([step] * (TILE // 128), axis=1)

        @pl.loop(0, cols // TILE)
        def _(t):
            tile = pl.ds(pl.multiple_of(t * TILE, TILE), TILE)
            part = blocks[pl.ds(2 * c, 2), :, tile].reshape(depth, TILE)
            term = jnp.dot(stacked[0 : 2 * count], part, preferred_element_type=jnp.float32)
            off_ref[span, tile] += step * (term[:count] + term[count:])

    relay(1)
    for d in range(2):
        panel_arrived(others[d] * 2 + core)
        panel_twin(d).start()
    relay(2)
    panel_arrived(others[2] * 2 + core)
    panel_twin(2).start()
    panel_arrived(twin)
    for d in range(3):
        panel_arrived(others[d] * 2 + (1 - core))

    @pl.loop(0, n)
    def _(c):
        @pl.when((c <= z + 2) & (c >= z - 2))
        def _():
            widen(c)
            accumulate(c, 0, rows)

    end = (z == 0) | (z == n - 1)
    last = n - 1 - z

    @pl.when(z == n - 1)
    def _():
        right_scale(last).wait_recv()

    @pl.when(z == 0)
    def _():
        left_scale(last).wait_recv()

    @pl.when(end)
    def _():
        widen(last)

    @pl.loop(0, pieces)
    def _(p):
        first = pl.multiple_of(p * PIECE, PIECE)
        span = pl.ds(first, PIECE)

        @pl.when(z == n - 1)
        def _():
            right_piece(last, p).wait_recv()

        @pl.when(z == 0)
        def _():
            left_piece(last, p).wait_recv()

        @pl.when(end)
        def _():
            accumulate(last, first, PIECE)

        off = -(off_ref[span, :] * mask_ref[...])
        off_ref[span, :] = off
        high = off.astype(jnp.bfloat16)
        low = (off - high.astype(jnp.float32)).astype(jnp.bfloat16)
        own = blocks[me, span, :]
        for k in range(cols // B):
            part = slice(k * B, (k + 1) * B)
            left = jnp.concatenate([own[:, part]] * 2, axis=0)
            both = jnp.concatenate([high[:, part], low[:, part]], axis=0)
            term = lax.dot_general(
                left, both, (((0,), (0,)), ((), ())), preferred_element_type=jnp.float32
            )
            partial[:, :, part] += term.reshape(8, B // 8, B)

    def to_twin(c):
        return far(partial.at[2 * c + (1 - core)], from_twin.at[c], t_send.at[c], t_recv.at[c], twin, z)

    def to_chip(d):
        return far(
            chip_sum.at[others[d]], from_chips.at[d], c_send.at[d], c_recv.at[d],
            others[d] * 2 + core, z,
        )

    order = (others[2], others[0], others[1], chip)
    for c in order:
        to_twin(c).start()
    for d in (2, 0, 1):
        c = others[d]
        to_twin(c).wait_recv()
        chip_sum[c] = partial[2 * c + core] + from_twin[c]
        to_chip(d).start()
    to_twin(chip).wait_recv()
    total = diag_ref[...] - (partial[me] + from_twin[chip])
    for d in (0, 1, 2):
        to_chip(d).wait_recv()
        total = total - from_chips[d]
    new_ref[...] = total

    for c in order:
        to_twin(c).wait_send()
    for d in range(3):
        to_chip(d).wait_send()
        panel_to(d).wait_send()
    for d in range(4):
        panel_twin(d).wait_send()
    for s in range(3):
        @pl.when((z >= s) & (z < n - 1))
        def _():
            right_scale(z - s).wait_send()

            @pl.loop(0, pieces)
            def _(p):
                right_piece(z - s, p).wait_send()

        @pl.when((z + s < n) & (z > 0))
        def _():
            left_scale(z + s).wait_send()

            @pl.loop(0, pieces)
            def _(p):
                left_piece(z + s, p).wait_send()


def fused_body(inverse_blocks, panel, diag_inverse, members, counts):
    rows_dev, cols_dev = panel.shape
    depth = inverse_blocks.shape[1]
    sup_count = cols_dev // B
    shards = lax.axis_size("col")
    pieces = rows_dev // PIECE
    mask = column_masks(members, counts, lax.axis_index("row"), lax.axis_index("col") * sup_count, sup_count)
    share = diag_inverse.shape[0]
    vmem = pl.BlockSpec(memory_space=pltpu.VMEM)
    dma = pltpu.SemaphoreType.DMA
    return pl.pallas_call(
        fused_kernel,
        out_shape=(
            jax.ShapeDtypeStruct((rows_dev, cols_dev), jnp.float32),
            jax.ShapeDtypeStruct((share, cols_dev), jnp.float32),
        ),
        in_specs=[vmem] * 4,
        out_specs=(vmem, vmem),
        scratch_shapes=[
            pltpu.VMEM((shards, rows_dev, depth), jnp.int16),
            pltpu.VMEM((shards, 8, rows_dev), jnp.float32),
            pltpu.VMEM((rows_dev, 128), jnp.float32),
            pltpu.VMEM((8, rows_dev, cols_dev), jnp.bfloat16),
            pltpu.VMEM((2 * rows_dev, depth), jnp.bfloat16),
            pltpu.VMEM((8, share, cols_dev), jnp.float32),
            pltpu.VMEM((4, share, cols_dev), jnp.float32),
            pltpu.VMEM((4, share, cols_dev), jnp.float32),
            pltpu.VMEM((3, share, cols_dev), jnp.float32),
            dma((shards, pieces)), dma((shards, pieces)), dma((shards, pieces)),
            dma((shards,)), dma((shards,)), dma((shards,)),
            dma((8,)), dma((3,)), dma((4,)), dma((4,)), dma((4,)), dma((3,)), dma((3,)),
        ],
        compiler_params=pltpu.CompilerParams(
            collective_id=0, has_side_effects=True, vmem_limit_bytes=56 * 1024 * 1024
        ),
    )(inverse_blocks, panel, mask[None, :], diag_inverse)


def body(inverse_blocks, panel, diag_inverse, members, counts):
    rows_dev, cols_dev = panel.shape
    sup_count = cols_dev // B
    depth = inverse_blocks.shape[1]
    ancestor = lax.axis_index("row") * rows_dev // B
    column_mask = column_masks(members, counts, ancestor, lax.axis_index("col") * sup_count, sup_count)
    masked = panel * column_mask.astype(jnp.bfloat16)[None, :]
    coded, scale = quantize(inverse_blocks)
    coded_all = lax.all_gather(coded, "col", axis=0, tiled=False)
    scale_all = lax.all_gather(scale, "col", axis=0, tiled=False)
    masked_all = lax.all_gather(masked, "row", axis=0, tiled=True)
    running = jnp.zeros((rows_dev, cols_dev), jnp.float32)
    for shard in range(coded_all.shape[0]):
        high, low = split_code(coded_all[shard])
        part = masked_all[shard * depth : (shard + 1) * depth]
        term = jnp.dot(high, part, preferred_element_type=jnp.float32) + jnp.dot(
            low, part, preferred_element_type=jnp.float32
        )
        running = running + scale_all[shard] * term
    offdiag = -(running * column_mask[None, :])
    off_high = lax.reduce_precision(offdiag, 8, 7)
    off_low = (offdiag - off_high).astype(jnp.bfloat16).reshape(rows_dev, sup_count, B)
    off_high = off_high.astype(jnp.bfloat16).reshape(rows_dev, sup_count, B)
    masked_blocks = masked.reshape(rows_dev, sup_count, B)
    diag_terms = jnp.einsum(
        "ikc,ikd->ckd", masked_blocks, off_high, preferred_element_type=jnp.float32
    ) + jnp.einsum("ikc,ikd->ckd", masked_blocks, off_low, preferred_element_type=jnp.float32)
    summed = lax.psum_scatter(
        diag_terms.reshape(B, sup_count * B), "row", scatter_dimension=0, tiled=True
    )
    return (offdiag, diag_inverse - summed)


def solution(mesh):
    fits = mesh.shape["row"] == 8 and mesh.shape["col"] == 4
    return jax.shard_map(
        fused_body if fits else body,
        mesh=mesh,
        in_specs=(P("row", "col"), P("row", "col"), P("row", "col"), P(), P()),
        out_specs=(P("row", "col"), P("row", "col")),
        check_vma=False,
    )
```

```python
import jax
import jax.numpy as jnp
from jax import lax
from jax.experimental import pallas as pl
from jax.experimental.pallas import tpu as pltpu
from jax.sharding import PartitionSpec as P

B = 512


def quantize(block):
    peak = jnp.max(jnp.abs(block), axis=1, keepdims=True)
    live = peak > 1e-30
    safe = jnp.where(live, peak, 1.0)
    coded = jnp.round(block * (32767.0 / safe)).astype(jnp.int16)
    return jnp.where(live, coded, 0), safe * (1.0 / 32767.0)


def split_code(coded):
    wide = coded.astype(jnp.int32)
    high = (wide + 64) & -128
    return high.astype(jnp.bfloat16), (wide - high).astype(jnp.bfloat16)


def column_masks(members, counts, ancestor, first_sup, sup_count):
    local_members = lax.dynamic_slice_in_dim(members, first_sup, sup_count, 0)
    local_counts = lax.dynamic_slice_in_dim(counts, first_sup, sup_count, 0)
    slot_index = jnp.arange(members.shape[1], dtype=jnp.int32)
    live_slot = slot_index[None, :] < local_counts[:, None]
    row_mask = jnp.sum(
        jnp.where((local_members == ancestor) & live_slot, 1.0, 0.0).astype(jnp.float32), axis=1
    )
    return jnp.repeat(row_mask, B)


MESH = pl.DeviceIdType.MESH
PIECE = 128
TILE = 256


def fused_kernel(
    inv_ref, panel_ref, diag_ref, members_ref, counts_ref, off_ref, new_ref,
    coded, scales, wide_scale, blocks, stacked, partial, from_twin, chip_sum, from_chips,
    late, late_partial, late_twin, late_sum, late_code, late_scale, code_in, scale_in, late_wide,
    a_recv, a_right, a_left, s_recv, s_right, s_left,
    p_recv, p_send, p_twin, t_recv, t_send, c_recv, c_send,
    lt_recv, lt_send, lc_recv, lc_send, ls_recv, ls_send,
):
    n = coded.shape[0]
    rows, depth = inv_ref.shape
    cols = panel_ref.shape[1]
    pieces = rows // PIECE
    me = lax.axis_index("row")
    z = lax.axis_index("col")
    chip, core = lax.div(me, 2), lax.rem(me, 2)
    y, x = lax.div(chip, 2), lax.rem(chip, 2)
    twin = chip * 2 + (1 - core)
    others = (y * 2 + (1 - x), (1 - y) * 2 + x, (1 - y) * 2 + (1 - x))

    def far(src, dst, send, recv, row, col):
        return pltpu.make_async_remote_copy(
            src_ref=src, dst_ref=dst, send_sem=send, recv_sem=recv,
            device_id=(row, col), device_id_type=MESH,
        )

    def right_piece(c, p):
        ref = coded.at[c, pl.ds(pl.multiple_of(p * PIECE, PIECE), PIECE)]
        return far(ref, ref, a_right.at[c, p], a_recv.at[c, p], me, z + 1)

    def left_piece(c, p):
        ref = coded.at[c, pl.ds(pl.multiple_of(p * PIECE, PIECE), PIECE)]
        return far(ref, ref, a_left.at[c, p], a_recv.at[c, p], me, z - 1)

    def right_scale(c):
        return far(scales.at[c], scales.at[c], s_right.at[c], s_recv.at[c], me, z + 1)

    def left_scale(c):
        return far(scales.at[c], scales.at[c], s_left.at[c], s_recv.at[c], me, z - 1)

    def panel_to(d):
        return far(blocks.at[me], blocks.at[me], p_send.at[d], p_recv.at[me], others[d] * 2 + core, z)

    def panel_twin(d):
        r = me if d == 3 else others[d] * 2 + core
        return far(blocks.at[r], blocks.at[r], p_twin.at[d], p_recv.at[r], twin, z)

    def panel_arrived(r):
        far(blocks.at[r], blocks.at[r], p_twin.at[0], p_recv.at[r], twin, z).wait_recv()

    barrier = pltpu.get_barrier_semaphore()
    for row in [twin] + [o * 2 + core for o in others]:
        pl.semaphore_signal(barrier, inc=1, device_id=(row, z), device_id_type=MESH)

    @pl.when(z > 0)
    def _():
        pl.semaphore_signal(barrier, inc=1, device_id=(me, z - 1), device_id_type=MESH)

    @pl.when(z < n - 1)
    def _():
        pl.semaphore_signal(barrier, inc=1, device_id=(me, z + 1), device_id_type=MESH)

    sup_count = cols // B
    masks = []
    for k in range(sup_count):
        sup = z * sup_count + k
        hit = jnp.int32(0)
        for slot in range(members_ref.shape[1]):
            match = jnp.where(members_ref[sup, slot] == me, 1, 0)
            hit += match * jnp.where(slot < counts_ref[sup], 1, 0)
        masks.append(jnp.broadcast_to(hit.astype(jnp.float32), (1, B)))
    mask = jnp.concatenate(masks, axis=1)

    block = inv_ref[...]
    peak = jnp.max(jnp.abs(block), axis=1, keepdims=True)
    live = peak > 1e-33
    safe = jnp.where(live, peak, 1.0)
    ratio = jnp.where(live, 32767.0 / safe, 0.0)
    ready = block * ratio
    ready = ready + jnp.where(ready >= 0.0, 0.5, -0.5)
    coded[z] = ready.astype(jnp.int32).astype(jnp.int16)
    step = jnp.broadcast_to(safe * (1.0 / 32767.0), (rows, 128))
    scales[z] = step.T[:8]
    blocks[me] = panel_ref[...] * mask.astype(jnp.bfloat16)

    pl.semaphore_wait(barrier, 4 + jnp.where(z > 0, 1, 0) + jnp.where(z < n - 1, 1, 0))

    @pl.when(z < n - 1)
    def _():
        right_scale(z).start()

        @pl.loop(0, pieces)
        def _(p):
            right_piece(z, p).start()

    @pl.when(z > 0)
    def _():
        left_scale(z).start()

        @pl.loop(0, pieces)
        def _(p):
            left_piece(z, p).start()

    panel_twin(3).start()
    for d in range(3):
        panel_to(d).start()
    off_ref[...] = jnp.zeros_like(off_ref)
    partial[...] = jnp.zeros_like(partial)

    def relay(s):
        @pl.loop(0, pieces)
        def _(p):
            @pl.when(z >= s)
            def _():
                @pl.when(p == 0)
                def _():
                    right_scale(z - s).wait_recv()

                right_piece(z - s, p).wait_recv()

                @pl.when(z < n - 1)
                def _():
                    @pl.when(p == 0)
                    def _():
                        right_scale(z - s).start()

                    right_piece(z - s, p).start()

            @pl.when(z + s < n)
            def _():
                @pl.when(p == 0)
                def _():
                    left_scale(z + s).wait_recv()

                left_piece(z + s, p).wait_recv()

                @pl.when(z > 0)
                def _():
                    @pl.when(p == 0)
                    def _():
                        left_scale(z + s).start()

                    left_piece(z + s, p).start()

    def widen(c):
        eight = scales[c]
        wide_scale[...] = jnp.concatenate([eight] * 16, axis=0).T

    def accumulate(c, first, count, into, where):
        span = pl.ds(first, count)
        code = coded[c, span, :].astype(jnp.int32)
        high = (code + 64) & -128
        stacked[0:count] = high.astype(jnp.float32).astype(jnp.bfloat16)
        stacked[count : 2 * count] = (code - high).astype(jnp.float32).astype(jnp.bfloat16)
        step = wide_scale[span, :]
        step = jnp.concatenate([step] * (TILE // 128), axis=1)

        @pl.loop(0, cols // TILE)
        def _(t):
            tile = pl.ds(pl.multiple_of(t * TILE, TILE), TILE)
            part = blocks[pl.ds(2 * c, 2), :, tile].reshape(depth, TILE)
            term = jnp.dot(stacked[0 : 2 * count], part, preferred_element_type=jnp.float32)
            into[where, tile] += step * (term[:count] + term[count:])

    relay(1)
    for d in range(2):
        panel_arrived(others[d] * 2 + core)
        panel_twin(d).start()
    relay(2)
    panel_arrived(others[2] * 2 + core)
    panel_twin(2).start()
    panel_arrived(twin)
    for d in range(3):
        panel_arrived(others[d] * 2 + (1 - core))

    @pl.loop(0, n)
    def _(c):
        @pl.when((c <= z + 2) & (c >= z - 2))
        def _():
            widen(c)
            accumulate(c, 0, rows, off_ref, pl.ds(0, rows))

    def diag_term(value, span, into):
        high = value.astype(jnp.bfloat16)
        low = (value - high.astype(jnp.float32)).astype(jnp.bfloat16)
        own = blocks[me, span, :]
        for k in range(sup_count):
            part = slice(k * B, (k + 1) * B)
            left = jnp.concatenate([own[:, part]] * 2, axis=0)
            both = jnp.concatenate([high[:, part], low[:, part]], axis=0)
            term = lax.dot_general(
                left, both, (((0,), (0,)), ((), ())), preferred_element_type=jnp.float32
            )
            into[:, :, part] += term.reshape(8, B // 8, B)

    @pl.loop(0, pieces)
    def _(p):
        span = pl.ds(pl.multiple_of(p * PIECE, PIECE), PIECE)
        diag_term(off_ref[span, :], span, partial)

    def to_twin(c):
        return far(partial.at[2 * c + (1 - core)], from_twin.at[c], t_send.at[c], t_recv.at[c], twin, z)

    def to_chip(d):
        return far(
            chip_sum.at[others[d]], from_chips.at[d], c_send.at[d], c_recv.at[d],
            others[d] * 2 + core, z,
        )

    def late_to_twin(c):
        return far(
            late_partial.at[2 * c + (1 - core)], late_twin.at[c], lt_send.at[c], lt_recv.at[c], twin, z
        )

    def late_to_chip(d):
        return far(
            late_code.at[others[d]], code_in.at[d], lc_send.at[d], lc_recv.at[d],
            others[d] * 2 + core, z,
        )

    def late_scale_to_chip(d):
        return far(late_scale, scale_in.at[d], ls_send.at[d], ls_recv.at[d], others[d] * 2 + core, z)

    order = (others[2], others[0], others[1], chip)
    for c in order:
        to_twin(c).start()
    late_partial[...] = jnp.zeros_like(late_partial)
    for d in (2, 0, 1):
        c = others[d]
        to_twin(c).wait_recv()
        chip_sum[c] = partial[2 * c + core] + from_twin[c]
        to_chip(d).start()
    to_twin(chip).wait_recv()
    new_ref[...] = diag_ref[...] + (partial[me] + from_twin[chip])

    end = (z == 0) | (z == n - 1)
    last = n - 1 - z

    @pl.when(z == n - 1)
    def _():
        right_scale(last).wait_recv()

    @pl.when(z == 0)
    def _():
        left_scale(last).wait_recv()

    @pl.when(end)
    def _():
        widen(last)

    @pl.loop(0, pieces)
    def _(p):
        first = pl.multiple_of(p * PIECE, PIECE)
        span = pl.ds(first, PIECE)

        @pl.when(z == n - 1)
        def _():
            right_piece(last, p).wait_recv()

        @pl.when(z == 0)
        def _():
            left_piece(last, p).wait_recv()

        late[...] = jnp.zeros_like(late)

        @pl.when(end)
        def _():
            accumulate(last, first, PIECE, late, pl.ds(0, PIECE))
            diag_term(late[...], span, late_partial)

        off_ref[span, :] = -((off_ref[span, :] + late[...]) * mask)

    @pl.when(end)
    def _():
        for c in order:
            late_to_twin(c).start()
        for d in range(3):
            to_chip(d).wait_recv()
            new_ref[...] += from_chips[d]
        for d in (2, 0, 1):
            c = others[d]
            late_to_twin(c).wait_recv()
            late_sum[c] = late_partial[2 * c + core] + late_twin[c]
        late_to_twin(chip).wait_recv()
        late_sum[chip] = jnp.zeros(late_sum.shape[1:], jnp.float32)
        share = late_sum.shape[1]
        value = late_sum[...].reshape(4 * share, cols)
        top = jnp.max(jnp.abs(value), axis=1, keepdims=True)
        some = top > 1e-33
        held = jnp.where(some, top, 1.0)
        ready = value * jnp.where(some, 32767.0 / held, 0.0)
        ready = ready + jnp.where(ready >= 0.0, 0.5, -0.5)
        late_code[...] = ready.astype(jnp.int32).astype(jnp.int16).reshape(4, share, cols)
        late_scale[...] = jnp.broadcast_to(held * (1.0 / 32767.0), (4 * share, 128)).T[:8]
        for d in (2, 0, 1):
            late_to_chip(d).start()
            late_scale_to_chip(d).start()
        new_ref[...] += late_partial[me] + late_twin[chip]
        for d in (0, 1, 2):
            late_scale_to_chip(d).wait_recv()
            late_to_chip(d).wait_recv()
            late_wide[...] = jnp.concatenate([scale_in[d]] * 16, axis=0).T
            unit = late_wide[pl.ds(pl.multiple_of(chip * share, share), share), :]
            unit = jnp.concatenate([unit] * (cols // 128), axis=1)
            new_ref[...] += code_in[d].astype(jnp.int32).astype(jnp.float32) * unit
        for c in order:
            late_to_twin(c).wait_send()
        for d in range(3):
            late_to_chip(d).wait_send()
            late_scale_to_chip(d).wait_send()

    @pl.when(jnp.logical_not(end))
    def _():
        for d in range(3):
            to_chip(d).wait_recv()
            new_ref[...] += from_chips[d]

    for c in order:
        to_twin(c).wait_send()
    for d in range(3):
        to_chip(d).wait_send()
        panel_to(d).wait_send()
    for d in range(4):
        panel_twin(d).wait_send()
    for s in range(3):
        @pl.when((z >= s) & (z < n - 1))
        def _():
            right_scale(z - s).wait_send()

            @pl.loop(0, pieces)
            def _(p):
                right_piece(z - s, p).wait_send()

        @pl.when((z + s < n) & (z > 0))
        def _():
            left_scale(z + s).wait_send()

            @pl.loop(0, pieces)
            def _(p):
                left_piece(z + s, p).wait_send()


def fused_body(inverse_blocks, panel, diag_inverse, members, counts):
    rows_dev, cols_dev = panel.shape
    depth = inverse_blocks.shape[1]
    shards = lax.axis_size("col")
    pieces = rows_dev // PIECE
    share = diag_inverse.shape[0]
    vmem = pl.BlockSpec(memory_space=pltpu.VMEM)
    dma = pltpu.SemaphoreType.DMA
    return pl.pallas_call(
        fused_kernel,
        out_shape=(
            jax.ShapeDtypeStruct((rows_dev, cols_dev), jnp.float32),
            jax.ShapeDtypeStruct((share, cols_dev), jnp.float32),
        ),
        in_specs=[vmem] * 3 + [pl.BlockSpec(memory_space=pltpu.SMEM)] * 2,
        out_specs=(vmem, vmem),
        scratch_shapes=[
            pltpu.VMEM((shards, rows_dev, depth), jnp.int16),
            pltpu.VMEM((shards, 8, rows_dev), jnp.float32),
            pltpu.VMEM((rows_dev, 128), jnp.float32),
            pltpu.VMEM((8, rows_dev, cols_dev), jnp.bfloat16),
            pltpu.VMEM((2 * rows_dev, depth), jnp.bfloat16),
            pltpu.VMEM((8, share, cols_dev), jnp.float32),
            pltpu.VMEM((4, share, cols_dev), jnp.float32),
            pltpu.VMEM((4, share, cols_dev), jnp.float32),
            pltpu.VMEM((3, share, cols_dev), jnp.float32),
            pltpu.VMEM((PIECE, cols_dev), jnp.float32),
            pltpu.VMEM((8, share, cols_dev), jnp.float32),
            pltpu.VMEM((4, share, cols_dev), jnp.float32),
            pltpu.VMEM((4, share, cols_dev), jnp.float32),
            pltpu.VMEM((4, share, cols_dev), jnp.int16),
            pltpu.VMEM((8, 4 * share), jnp.float32),
            pltpu.VMEM((3, share, cols_dev), jnp.int16),
            pltpu.VMEM((3, 8, 4 * share), jnp.float32),
            pltpu.VMEM((4 * share, 128), jnp.float32),
            dma((shards, pieces)), dma((shards, pieces)), dma((shards, pieces)),
            dma((shards,)), dma((shards,)), dma((shards,)),
            dma((8,)), dma((3,)), dma((4,)), dma((4,)), dma((4,)), dma((3,)), dma((3,)),
            dma((4,)), dma((4,)), dma((3,)), dma((3,)), dma((3,)), dma((3,)),
        ],
        compiler_params=pltpu.CompilerParams(
            collective_id=0, has_side_effects=True, vmem_limit_bytes=56 * 1024 * 1024
        ),
    )(inverse_blocks, panel, diag_inverse, members, counts)


def body(inverse_blocks, panel, diag_inverse, members, counts):
    rows_dev, cols_dev = panel.shape
    sup_count = cols_dev // B
    depth = inverse_blocks.shape[1]
    ancestor = lax.axis_index("row") * rows_dev // B
    column_mask = column_masks(members, counts, ancestor, lax.axis_index("col") * sup_count, sup_count)
    masked = panel * column_mask.astype(jnp.bfloat16)[None, :]
    coded, scale = quantize(inverse_blocks)
    coded_all = lax.all_gather(coded, "col", axis=0, tiled=False)
    scale_all = lax.all_gather(scale, "col", axis=0, tiled=False)
    masked_all = lax.all_gather(masked, "row", axis=0, tiled=True)
    running = jnp.zeros((rows_dev, cols_dev), jnp.float32)
    for shard in range(coded_all.shape[0]):
        high, low = split_code(coded_all[shard])
        part = masked_all[shard * depth : (shard + 1) * depth]
        term = jnp.dot(high, part, preferred_element_type=jnp.float32) + jnp.dot(
            low, part, preferred_element_type=jnp.float32
        )
        running = running + scale_all[shard] * term
    offdiag = -(running * column_mask[None, :])
    off_high = lax.reduce_precision(offdiag, 8, 7)
    off_low = (offdiag - off_high).astype(jnp.bfloat16).reshape(rows_dev, sup_count, B)
    off_high = off_high.astype(jnp.bfloat16).reshape(rows_dev, sup_count, B)
    masked_blocks = masked.reshape(rows_dev, sup_count, B)
    diag_terms = jnp.einsum(
        "ikc,ikd->ckd", masked_blocks, off_high, preferred_element_type=jnp.float32
    ) + jnp.einsum("ikc,ikd->ckd", masked_blocks, off_low, preferred_element_type=jnp.float32)
    summed = lax.psum_scatter(
        diag_terms.reshape(B, sup_count * B), "row", scatter_dimension=0, tiled=True
    )
    return (offdiag, diag_inverse - summed)


def solution(mesh):
    fits = mesh.shape["row"] == 8 and mesh.shape["col"] == 4
    return jax.shard_map(
        fused_body if fits else body,
        mesh=mesh,
        in_specs=(P("row", "col"), P("row", "col"), P("row", "col"), P(), P()),
        out_specs=(P("row", "col"), P("row", "col")),
        check_vma=False,
    )
```

```python
import jax
import jax.numpy as jnp
from jax import lax
from jax.experimental import pallas as pl
from jax.experimental.pallas import tpu as pltpu
from jax.sharding import PartitionSpec as P

B = 512


def quantize(block):
    peak = jnp.max(jnp.abs(block), axis=1, keepdims=True)
    live = peak > 1e-30
    safe = jnp.where(live, peak, 1.0)
    coded = jnp.round(block * (32767.0 / safe)).astype(jnp.int16)
    return jnp.where(live, coded, 0), safe * (1.0 / 32767.0)


def split_code(coded):
    wide = coded.astype(jnp.int32)
    high = (wide + 64) & -128
    return high.astype(jnp.bfloat16), (wide - high).astype(jnp.bfloat16)


def column_masks(members, counts, ancestor, first_sup, sup_count):
    local_members = lax.dynamic_slice_in_dim(members, first_sup, sup_count, 0)
    local_counts = lax.dynamic_slice_in_dim(counts, first_sup, sup_count, 0)
    slot_index = jnp.arange(members.shape[1], dtype=jnp.int32)
    live_slot = slot_index[None, :] < local_counts[:, None]
    row_mask = jnp.sum(
        jnp.where((local_members == ancestor) & live_slot, 1.0, 0.0).astype(jnp.float32), axis=1
    )
    return jnp.repeat(row_mask, B)


MESH = pl.DeviceIdType.MESH
PIECE = 128
TILE = 256


def fused_kernel(
    inv_ref, panel_ref, diag_ref, members_ref, counts_ref, off_ref, new_ref,
    coded, scales, wide_scale, blocks, stacked, partial, from_twin, chip_sum, from_chips,
    late, late_partial, late_twin, late_sum, late_code, late_scale, code_in, scale_in, late_wide,
    a_recv, a_right, a_left, s_recv, s_right, s_left,
    p_recv, p_send, p_pass, p_twin, t_recv, t_send, c_recv, c_send,
    lt_recv, lt_send, lc_recv, lc_send, ls_recv, ls_send,
):
    n = coded.shape[0]
    rows, depth = inv_ref.shape
    cols = panel_ref.shape[1]
    pieces = rows // PIECE
    me = lax.axis_index("row")
    z = lax.axis_index("col")
    chip, core = lax.div(me, 2), lax.rem(me, 2)
    y, x = lax.div(chip, 2), lax.rem(chip, 2)
    twin = chip * 2 + (1 - core)
    others = (y * 2 + (1 - x), (1 - y) * 2 + x, (1 - y) * 2 + (1 - x))

    def far(src, dst, send, recv, row, col):
        return pltpu.make_async_remote_copy(
            src_ref=src, dst_ref=dst, send_sem=send, recv_sem=recv,
            device_id=(row, col), device_id_type=MESH,
        )

    def right_piece(c, p):
        ref = coded.at[c, pl.ds(pl.multiple_of(p * PIECE, PIECE), PIECE)]
        return far(ref, ref, a_right.at[c, p], a_recv.at[c, p], me, z + 1)

    def left_piece(c, p):
        ref = coded.at[c, pl.ds(pl.multiple_of(p * PIECE, PIECE), PIECE)]
        return far(ref, ref, a_left.at[c, p], a_recv.at[c, p], me, z - 1)

    def right_scale(c):
        return far(scales.at[c], scales.at[c], s_right.at[c], s_recv.at[c], me, z + 1)

    def left_scale(c):
        return far(scales.at[c], scales.at[c], s_left.at[c], s_recv.at[c], me, z - 1)

    def half_of(r, h):
        return blocks.at[r, pl.ds(h * (rows // 2), rows // 2)]

    def panel_to(d, h):
        ref = half_of(me, h)
        return far(ref, ref, p_send.at[d, h], p_recv.at[me, h], others[d] * 2 + core, z)

    def panel_pass(d):
        r = others[1 - d] * 2 + core
        return far(half_of(r, d), half_of(r, d), p_pass.at[d], p_recv.at[r, d], others[d] * 2 + core, z)

    def panel_twin(d, h):
        r = me if d == 3 else others[d] * 2 + core
        return far(half_of(r, h), half_of(r, h), p_twin.at[d, h], p_recv.at[r, h], twin, z)

    def panel_arrived(r, h):
        far(half_of(r, h), half_of(r, h), p_twin.at[0, 0], p_recv.at[r, h], twin, z).wait_recv()

    barrier = pltpu.get_barrier_semaphore()
    for row in [twin] + [o * 2 + core for o in others]:
        pl.semaphore_signal(barrier, inc=1, device_id=(row, z), device_id_type=MESH)

    @pl.when(z > 0)
    def _():
        pl.semaphore_signal(barrier, inc=1, device_id=(me, z - 1), device_id_type=MESH)

    @pl.when(z < n - 1)
    def _():
        pl.semaphore_signal(barrier, inc=1, device_id=(me, z + 1), device_id_type=MESH)

    sup_count = cols // B
    masks = []
    for k in range(sup_count):
        sup = z * sup_count + k
        hit = jnp.int32(0)
        for slot in range(members_ref.shape[1]):
            match = jnp.where(members_ref[sup, slot] == me, 1, 0)
            hit += match * jnp.where(slot < counts_ref[sup], 1, 0)
        masks.append(jnp.broadcast_to(hit.astype(jnp.float32), (1, B)))
    mask = jnp.concatenate(masks, axis=1)

    block = inv_ref[...]
    peak = jnp.max(jnp.abs(block), axis=1, keepdims=True)
    live = peak > 1e-33
    safe = jnp.where(live, peak, 1.0)
    ratio = jnp.where(live, 32767.0 / safe, 0.0)
    ready = block * ratio
    ready = ready + jnp.where(ready >= 0.0, 0.5, -0.5)
    coded[z] = ready.astype(jnp.int32).astype(jnp.int16)
    step = jnp.broadcast_to(safe * (1.0 / 32767.0), (rows, 128))
    scales[z] = step.T[:8]
    blocks[me] = panel_ref[...] * mask.astype(jnp.bfloat16)

    pl.semaphore_wait(barrier, 4 + jnp.where(z > 0, 1, 0) + jnp.where(z < n - 1, 1, 0))

    @pl.when(z < n - 1)
    def _():
        right_scale(z).start()

        @pl.loop(0, pieces)
        def _(p):
            right_piece(z, p).start()

    @pl.when(z > 0)
    def _():
        left_scale(z).start()

        @pl.loop(0, pieces)
        def _(p):
            left_piece(z, p).start()

    for d, h in ((0, 1), (1, 0), (0, 0), (1, 1)):
        panel_to(d, h).start()
    for h in range(2):
        panel_twin(3, h).start()
    off_ref[...] = jnp.zeros_like(off_ref)
    partial[...] = jnp.zeros_like(partial)

    def relay(s):
        @pl.loop(0, pieces)
        def _(p):
            @pl.when(z >= s)
            def _():
                @pl.when(p == 0)
                def _():
                    right_scale(z - s).wait_recv()

                right_piece(z - s, p).wait_recv()

                @pl.when(z < n - 1)
                def _():
                    @pl.when(p == 0)
                    def _():
                        right_scale(z - s).start()

                    right_piece(z - s, p).start()

            @pl.when(z + s < n)
            def _():
                @pl.when(p == 0)
                def _():
                    left_scale(z + s).wait_recv()

                left_piece(z + s, p).wait_recv()

                @pl.when(z > 0)
                def _():
                    @pl.when(p == 0)
                    def _():
                        left_scale(z + s).start()

                    left_piece(z + s, p).start()

    def widen(c):
        eight = scales[c]
        wide_scale[...] = jnp.concatenate([eight] * 16, axis=0).T

    def accumulate(c, first, count, into, where):
        span = pl.ds(first, count)
        code = coded[c, span, :].astype(jnp.int32)
        high = (code + 64) & -128
        stacked[0:count] = high.astype(jnp.float32).astype(jnp.bfloat16)
        stacked[count : 2 * count] = (code - high).astype(jnp.float32).astype(jnp.bfloat16)
        step = wide_scale[span, :]
        step = jnp.concatenate([step] * (TILE // 128), axis=1)

        @pl.loop(0, cols // TILE)
        def _(t):
            tile = pl.ds(pl.multiple_of(t * TILE, TILE), TILE)
            part = blocks[pl.ds(2 * c, 2), :, tile].reshape(depth, TILE)
            term = jnp.dot(stacked[0 : 2 * count], part, preferred_element_type=jnp.float32)
            into[where, tile] += step * (term[:count] + term[count:])

    def accumulate_near(low, high):
        @pl.loop(0, n)
        def _(c):
            gap = jnp.where(c > z, c - z, z - c)

            @pl.when((gap >= low) & (gap <= high))
            def _():
                widen(c)
                accumulate(c, 0, rows, off_ref, pl.ds(0, rows))

    end = (z == 0) | (z == n - 1)
    last = n - 1 - z
    relay(1)
    for d in range(2):
        panel_arrived(others[1 - d] * 2 + core, d)
        panel_pass(d).start()
        panel_twin(1 - d, d).start()
    for d in range(2):
        panel_arrived(others[d] * 2 + core, d)
        panel_twin(d, d).start()
    for h in range(2):
        panel_arrived(others[2] * 2 + core, h)
        panel_twin(2, h).start()
    for h in range(2):
        panel_arrived(twin, h)
        for d in range(3):
            panel_arrived(others[d] * 2 + (1 - core), h)

    @pl.when(end)
    def _():
        accumulate_near(0, 1)

    relay(2)
    accumulate_near(jnp.where(end, 2, 0), 2)

    def diag_term(value, span, into):
        high = value.astype(jnp.bfloat16)
        low = (value - high.astype(jnp.float32)).astype(jnp.bfloat16)
        own = blocks[me, span, :]
        for k in range(sup_count):
            part = slice(k * B, (k + 1) * B)
            left = jnp.concatenate([own[:, part]] * 2, axis=0)
            both = jnp.concatenate([high[:, part], low[:, part]], axis=0)
            term = lax.dot_general(
                left, both, (((0,), (0,)), ((), ())), preferred_element_type=jnp.float32
            )
            into[:, :, part] += term.reshape(8, B // 8, B)

    @pl.loop(0, pieces)
    def _(p):
        span = pl.ds(pl.multiple_of(p * PIECE, PIECE), PIECE)
        diag_term(off_ref[span, :], span, partial)

    def to_twin(c):
        return far(partial.at[2 * c + (1 - core)], from_twin.at[c], t_send.at[c], t_recv.at[c], twin, z)

    def to_chip(d):
        return far(
            chip_sum.at[others[d]], from_chips.at[d], c_send.at[d], c_recv.at[d],
            others[d] * 2 + core, z,
        )

    def late_to_twin(c):
        return far(
            late_partial.at[2 * c + (1 - core)], late_twin.at[c], lt_send.at[c], lt_recv.at[c], twin, z
        )

    def late_to_chip(d):
        return far(
            late_code.at[others[d]], code_in.at[d], lc_send.at[d], lc_recv.at[d],
            others[d] * 2 + core, z,
        )

    def late_scale_to_chip(d):
        return far(late_scale, scale_in.at[d], ls_send.at[d], ls_recv.at[d], others[d] * 2 + core, z)

    order = (others[2], others[0], others[1], chip)
    for c in order:
        to_twin(c).start()
    late_partial[...] = jnp.zeros_like(late_partial)
    for d in (2, 0, 1):
        c = others[d]
        to_twin(c).wait_recv()
        chip_sum[c] = partial[2 * c + core] + from_twin[c]
        to_chip(d).start()
    to_twin(chip).wait_recv()
    new_ref[...] = diag_ref[...] + (partial[me] + from_twin[chip])

    @pl.when(z == n - 1)
    def _():
        right_scale(last).wait_recv()

    @pl.when(z == 0)
    def _():
        left_scale(last).wait_recv()

    @pl.when(end)
    def _():
        widen(last)

    @pl.loop(0, pieces)
    def _(p):
        first = pl.multiple_of(p * PIECE, PIECE)
        span = pl.ds(first, PIECE)

        @pl.when(z == n - 1)
        def _():
            right_piece(last, p).wait_recv()

        @pl.when(z == 0)
        def _():
            left_piece(last, p).wait_recv()

        late[...] = jnp.zeros_like(late)

        @pl.when(end)
        def _():
            accumulate(last, first, PIECE, late, pl.ds(0, PIECE))
            diag_term(late[...], span, late_partial)

        off_ref[span, :] = -((off_ref[span, :] + late[...]) * mask)

    @pl.when(end)
    def _():
        for c in order:
            late_to_twin(c).start()
        for d in range(3):
            to_chip(d).wait_recv()
            new_ref[...] += from_chips[d]
        for d in (2, 0, 1):
            c = others[d]
            late_to_twin(c).wait_recv()
            late_sum[c] = late_partial[2 * c + core] + late_twin[c]
        late_to_twin(chip).wait_recv()
        late_sum[chip] = jnp.zeros(late_sum.shape[1:], jnp.float32)
        share = late_sum.shape[1]
        value = late_sum[...].reshape(4 * share, cols)
        top = jnp.max(jnp.abs(value), axis=1, keepdims=True)
        some = top > 1e-33
        held = jnp.where(some, top, 1.0)
        ready = value * jnp.where(some, 32767.0 / held, 0.0)
        ready = ready + jnp.where(ready >= 0.0, 0.5, -0.5)
        late_code[...] = ready.astype(jnp.int32).astype(jnp.int16).reshape(4, share, cols)
        late_scale[...] = jnp.broadcast_to(held * (1.0 / 32767.0), (4 * share, 128)).T[:8]
        for d in (2, 0, 1):
            late_to_chip(d).start()
            late_scale_to_chip(d).start()
        new_ref[...] += late_partial[me] + late_twin[chip]
        for d in (0, 1, 2):
            late_scale_to_chip(d).wait_recv()
            late_to_chip(d).wait_recv()
            late_wide[...] = jnp.concatenate([scale_in[d]] * 16, axis=0).T
            unit = late_wide[pl.ds(pl.multiple_of(chip * share, share), share), :]
            unit = jnp.concatenate([unit] * (cols // 128), axis=1)
            new_ref[...] += code_in[d].astype(jnp.int32).astype(jnp.float32) * unit
        for c in order:
            late_to_twin(c).wait_send()
        for d in range(3):
            late_to_chip(d).wait_send()
            late_scale_to_chip(d).wait_send()

    @pl.when(jnp.logical_not(end))
    def _():
        for d in range(3):
            to_chip(d).wait_recv()
            new_ref[...] += from_chips[d]

    for c in order:
        to_twin(c).wait_send()
    for d in range(3):
        to_chip(d).wait_send()
    for h in range(2):
        panel_pass(h).wait_send()
        for d in range(2):
            panel_to(d, h).wait_send()
        for d in range(4):
            panel_twin(d, h).wait_send()
    for s in range(3):
        @pl.when((z >= s) & (z < n - 1))
        def _():
            right_scale(z - s).wait_send()

            @pl.loop(0, pieces)
            def _(p):
                right_piece(z - s, p).wait_send()

        @pl.when((z + s < n) & (z > 0))
        def _():
            left_scale(z + s).wait_send()

            @pl.loop(0, pieces)
            def _(p):
                left_piece(z + s, p).wait_send()


def fused_body(inverse_blocks, panel, diag_inverse, members, counts):
    rows_dev, cols_dev = panel.shape
    depth = inverse_blocks.shape[1]
    shards = lax.axis_size("col")
    pieces = rows_dev // PIECE
    share = diag_inverse.shape[0]
    vmem = pl.BlockSpec(memory_space=pltpu.VMEM)
    dma = pltpu.SemaphoreType.DMA
    return pl.pallas_call(
        fused_kernel,
        out_shape=(
            jax.ShapeDtypeStruct((rows_dev, cols_dev), jnp.float32),
            jax.ShapeDtypeStruct((share, cols_dev), jnp.float32),
        ),
        in_specs=[vmem] * 3 + [pl.BlockSpec(memory_space=pltpu.SMEM)] * 2,
        out_specs=(vmem, vmem),
        scratch_shapes=[
            pltpu.VMEM((shards, rows_dev, depth), jnp.int16),
            pltpu.VMEM((shards, 8, rows_dev), jnp.float32),
            pltpu.VMEM((rows_dev, 128), jnp.float32),
            pltpu.VMEM((8, rows_dev, cols_dev), jnp.bfloat16),
            pltpu.VMEM((2 * rows_dev, depth), jnp.bfloat16),
            pltpu.VMEM((8, share, cols_dev), jnp.float32),
            pltpu.VMEM((4, share, cols_dev), jnp.float32),
            pltpu.VMEM((4, share, cols_dev), jnp.float32),
            pltpu.VMEM((3, share, cols_dev), jnp.float32),
            pltpu.VMEM((PIECE, cols_dev), jnp.float32),
            pltpu.VMEM((8, share, cols_dev), jnp.float32),
            pltpu.VMEM((4, share, cols_dev), jnp.float32),
            pltpu.VMEM((4, share, cols_dev), jnp.float32),
            pltpu.VMEM((4, share, cols_dev), jnp.int16),
            pltpu.VMEM((8, 4 * share), jnp.float32),
            pltpu.VMEM((3, share, cols_dev), jnp.int16),
            pltpu.VMEM((3, 8, 4 * share), jnp.float32),
            pltpu.VMEM((4 * share, 128), jnp.float32),
            dma((shards, pieces)), dma((shards, pieces)), dma((shards, pieces)),
            dma((shards,)), dma((shards,)), dma((shards,)),
            dma((8, 2)), dma((2, 2)), dma((2,)), dma((4, 2)), dma((4,)), dma((4,)), dma((3,)), dma((3,)),
            dma((4,)), dma((4,)), dma((3,)), dma((3,)), dma((3,)), dma((3,)),
        ],
        compiler_params=pltpu.CompilerParams(
            collective_id=0, has_side_effects=True, vmem_limit_bytes=56 * 1024 * 1024
        ),
    )(inverse_blocks, panel, diag_inverse, members, counts)


def body(inverse_blocks, panel, diag_inverse, members, counts):
    rows_dev, cols_dev = panel.shape
    sup_count = cols_dev // B
    depth = inverse_blocks.shape[1]
    ancestor = lax.axis_index("row") * rows_dev // B
    column_mask = column_masks(members, counts, ancestor, lax.axis_index("col") * sup_count, sup_count)
    masked = panel * column_mask.astype(jnp.bfloat16)[None, :]
    coded, scale = quantize(inverse_blocks)
    coded_all = lax.all_gather(coded, "col", axis=0, tiled=False)
    scale_all = lax.all_gather(scale, "col", axis=0, tiled=False)
    masked_all = lax.all_gather(masked, "row", axis=0, tiled=True)
    running = jnp.zeros((rows_dev, cols_dev), jnp.float32)
    for shard in range(coded_all.shape[0]):
        high, low = split_code(coded_all[shard])
        part = masked_all[shard * depth : (shard + 1) * depth]
        term = jnp.dot(high, part, preferred_element_type=jnp.float32) + jnp.dot(
            low, part, preferred_element_type=jnp.float32
        )
        running = running + scale_all[shard] * term
    offdiag = -(running * column_mask[None, :])
    off_high = lax.reduce_precision(offdiag, 8, 7)
    off_low = (offdiag - off_high).astype(jnp.bfloat16).reshape(rows_dev, sup_count, B)
    off_high = off_high.astype(jnp.bfloat16).reshape(rows_dev, sup_count, B)
    masked_blocks = masked.reshape(rows_dev, sup_count, B)
    diag_terms = jnp.einsum(
        "ikc,ikd->ckd", masked_blocks, off_high, preferred_element_type=jnp.float32
    ) + jnp.einsum("ikc,ikd->ckd", masked_blocks, off_low, preferred_element_type=jnp.float32)
    summed = lax.psum_scatter(
        diag_terms.reshape(B, sup_count * B), "row", scatter_dimension=0, tiled=True
    )
    return (offdiag, diag_inverse - summed)


def solution(mesh):
    fits = mesh.shape["row"] == 8 and mesh.shape["col"] == 4
    return jax.shard_map(
        fused_body if fits else body,
        mesh=mesh,
        in_specs=(P("row", "col"), P("row", "col"), P("row", "col"), P(), P()),
        out_specs=(P("row", "col"), P("row", "col")),
        check_vma=False,
    )
```

```python
import jax
import jax.numpy as jnp
from jax import lax
from jax.experimental import pallas as pl
from jax.experimental.pallas import tpu as pltpu
from jax.sharding import PartitionSpec as P

B = 512


def quantize(block):
    peak = jnp.max(jnp.abs(block), axis=1, keepdims=True)
    live = peak > 1e-30
    safe = jnp.where(live, peak, 1.0)
    coded = jnp.round(block * (32767.0 / safe)).astype(jnp.int16)
    return jnp.where(live, coded, 0), safe * (1.0 / 32767.0)


def split_code(coded):
    wide = coded.astype(jnp.int32)
    high = (wide + 64) & -128
    return high.astype(jnp.bfloat16), (wide - high).astype(jnp.bfloat16)


def column_masks(members, counts, ancestor, first_sup, sup_count):
    local_members = lax.dynamic_slice_in_dim(members, first_sup, sup_count, 0)
    local_counts = lax.dynamic_slice_in_dim(counts, first_sup, sup_count, 0)
    slot_index = jnp.arange(members.shape[1], dtype=jnp.int32)
    live_slot = slot_index[None, :] < local_counts[:, None]
    row_mask = jnp.sum(
        jnp.where((local_members == ancestor) & live_slot, 1.0, 0.0).astype(jnp.float32), axis=1
    )
    return jnp.repeat(row_mask, B)


MESH = pl.DeviceIdType.MESH
PIECE = 128
TILE = 256


def fused_kernel(
    inv_hbm, panel_hbm, diag_hbm, members_hbm, counts_hbm, off_ref, new_ref,
    inv_ref, panel_ref, diag_ref, members_ref, counts_ref, load,
    coded, scales, wide_scale, blocks, stacked, partial, from_twin, chip_sum, from_chips,
    late, late_partial, late_twin, late_sum, late_code, late_scale, code_in, scale_in, late_wide,
    a_recv, a_right, a_left, s_recv, s_right, s_left,
    p_recv, p_send, p_pass, p_twin, t_recv, t_send, c_recv, c_send,
    lt_recv, lt_send, lc_recv, lc_send, ls_recv, ls_send,
):
    n = coded.shape[0]
    rows, depth = inv_hbm.shape
    cols = panel_hbm.shape[1]
    pieces = rows // PIECE
    me = lax.axis_index("row")
    z = lax.axis_index("col")
    chip, core = lax.div(me, 2), lax.rem(me, 2)
    y, x = lax.div(chip, 2), lax.rem(chip, 2)
    twin = chip * 2 + (1 - core)
    others = (y * 2 + (1 - x), (1 - y) * 2 + x, (1 - y) * 2 + (1 - x))

    def far(src, dst, send, recv, row, col):
        return pltpu.make_async_remote_copy(
            src_ref=src, dst_ref=dst, send_sem=send, recv_sem=recv,
            device_id=(row, col), device_id_type=MESH,
        )

    def rows_of(p):
        if isinstance(p, int):
            return pl.ds(p * PIECE, PIECE)
        return pl.ds(pl.multiple_of(p * PIECE, PIECE), PIECE)

    def right_piece(c, p):
        ref = coded.at[c, rows_of(p)]
        return far(ref, ref, a_right.at[c, p], a_recv.at[c, p], me, z + 1)

    def left_piece(c, p):
        ref = coded.at[c, rows_of(p)]
        return far(ref, ref, a_left.at[c, p], a_recv.at[c, p], me, z - 1)

    def right_scale(c):
        return far(scales.at[c], scales.at[c], s_right.at[c], s_recv.at[c], me, z + 1)

    def left_scale(c):
        return far(scales.at[c], scales.at[c], s_left.at[c], s_recv.at[c], me, z - 1)

    def half_of(r, h):
        return blocks.at[r, pl.ds(h * (rows // 2), rows // 2)]

    def panel_to(d, h):
        ref = half_of(me, h)
        return far(ref, ref, p_send.at[d, h], p_recv.at[me, h], others[d] * 2 + core, z)

    def panel_pass(d):
        r = others[1 - d] * 2 + core
        return far(half_of(r, d), half_of(r, d), p_pass.at[d], p_recv.at[r, d], others[d] * 2 + core, z)

    def panel_twin(d, h):
        r = me if d == 3 else others[d] * 2 + core
        return far(half_of(r, h), half_of(r, h), p_twin.at[d, h], p_recv.at[r, h], twin, z)

    def panel_arrived(r, h):
        far(half_of(r, h), half_of(r, h), p_twin.at[0, 0], p_recv.at[r, h], twin, z).wait_recv()

    loads = [
        pltpu.make_async_copy(src, dst, load.at[i])
        for i, (src, dst) in enumerate(
            (
                (inv_hbm, inv_ref), (members_hbm, members_ref), (counts_hbm, counts_ref),
                (panel_hbm, panel_ref), (diag_hbm, diag_ref),
            )
        )
    ]
    for copy in loads:
        copy.start()
    barrier = pltpu.get_barrier_semaphore()
    for row in [twin] + [o * 2 + core for o in others]:
        pl.semaphore_signal(barrier, inc=1, device_id=(row, z), device_id_type=MESH)

    @pl.when(z > 0)
    def _():
        pl.semaphore_signal(barrier, inc=1, device_id=(me, z - 1), device_id_type=MESH)

    @pl.when(z < n - 1)
    def _():
        pl.semaphore_signal(barrier, inc=1, device_id=(me, z + 1), device_id_type=MESH)

    loads[0].wait()
    peak = jnp.max(jnp.abs(inv_ref[...]), axis=1, keepdims=True)
    live = peak > 1e-33
    safe = jnp.where(live, peak, 1.0)
    ratio = jnp.where(live, 32767.0 / safe, 0.0)
    step = jnp.broadcast_to(safe * (1.0 / 32767.0), (rows, 128))
    scales[z] = step.T[:8]
    pl.semaphore_wait(barrier, 4 + jnp.where(z > 0, 1, 0) + jnp.where(z < n - 1, 1, 0))

    @pl.when(z < n - 1)
    def _():
        right_scale(z).start()

    @pl.when(z > 0)
    def _():
        left_scale(z).start()

    for p in range(pieces):
        span = slice(p * PIECE, (p + 1) * PIECE)
        ready = inv_ref[span, :] * ratio[span]
        ready = ready + jnp.where(ready >= 0.0, 0.5, -0.5)
        coded[z, span, :] = ready.astype(jnp.int32).astype(jnp.int16)

        @pl.when(z < n - 1)
        def _():
            right_piece(z, p).start()

        @pl.when(z > 0)
        def _():
            left_piece(z, p).start()

    for copy in loads[1:]:
        copy.wait()
    sup_count = cols // B
    masks = []
    for k in range(sup_count):
        sup = z * sup_count + k
        hit = jnp.int32(0)
        for slot in range(members_ref.shape[1]):
            match = jnp.where(members_ref[sup, slot] == me, 1, 0)
            hit += match * jnp.where(slot < counts_ref[sup], 1, 0)
        masks.append(jnp.broadcast_to(hit.astype(jnp.float32), (1, B)))
    mask = jnp.concatenate(masks, axis=1)

    blocks[me] = panel_ref[...] * mask.astype(jnp.bfloat16)
    for d, h in ((0, 1), (1, 0), (0, 0), (1, 1)):
        panel_to(d, h).start()
    for h in range(2):
        panel_twin(3, h).start()
    off_ref[...] = jnp.zeros_like(off_ref)
    partial[...] = jnp.zeros_like(partial)

    def relay(s):
        @pl.loop(0, pieces)
        def _(p):
            @pl.when(z >= s)
            def _():
                @pl.when(p == 0)
                def _():
                    right_scale(z - s).wait_recv()

                right_piece(z - s, p).wait_recv()

                @pl.when(z < n - 1)
                def _():
                    @pl.when(p == 0)
                    def _():
                        right_scale(z - s).start()

                    right_piece(z - s, p).start()

            @pl.when(z + s < n)
            def _():
                @pl.when(p == 0)
                def _():
                    left_scale(z + s).wait_recv()

                left_piece(z + s, p).wait_recv()

                @pl.when(z > 0)
                def _():
                    @pl.when(p == 0)
                    def _():
                        left_scale(z + s).start()

                    left_piece(z + s, p).start()

    def widen(c):
        eight = scales[c]
        wide_scale[...] = jnp.concatenate([eight] * 16, axis=0).T

    def accumulate(c, first, count, into, where):
        span = pl.ds(first, count)
        code = coded[c, span, :].astype(jnp.int32)
        high = (code + 64) & -128
        stacked[0:count] = high.astype(jnp.float32).astype(jnp.bfloat16)
        stacked[count : 2 * count] = (code - high).astype(jnp.float32).astype(jnp.bfloat16)
        step = wide_scale[span, :]
        step = jnp.concatenate([step] * (TILE // 128), axis=1)

        @pl.loop(0, cols // TILE)
        def _(t):
            tile = pl.ds(pl.multiple_of(t * TILE, TILE), TILE)
            part = blocks[pl.ds(2 * c, 2), :, tile].reshape(depth, TILE)
            term = jnp.dot(stacked[0 : 2 * count], part, preferred_element_type=jnp.float32)
            into[where, tile] += step * (term[:count] + term[count:])

    def accumulate_near(low, high):
        @pl.loop(0, n)
        def _(c):
            gap = jnp.where(c > z, c - z, z - c)

            @pl.when((gap >= low) & (gap <= high))
            def _():
                widen(c)
                accumulate(c, 0, rows, off_ref, pl.ds(0, rows))

    end = (z == 0) | (z == n - 1)
    last = n - 1 - z
    relay(1)
    for d in range(2):
        panel_arrived(others[1 - d] * 2 + core, d)
        panel_pass(d).start()
        panel_twin(1 - d, d).start()
    for d in range(2):
        panel_arrived(others[d] * 2 + core, d)
        panel_twin(d, d).start()
    for h in range(2):
        panel_arrived(others[2] * 2 + core, h)
        panel_twin(2, h).start()
    for h in range(2):
        panel_arrived(twin, h)
        for d in range(3):
            panel_arrived(others[d] * 2 + (1 - core), h)

    @pl.when(end)
    def _():
        accumulate_near(0, 1)

    relay(2)
    accumulate_near(jnp.where(end, 2, 0), 2)

    def diag_term(value, span, into):
        high = value.astype(jnp.bfloat16)
        low = (value - high.astype(jnp.float32)).astype(jnp.bfloat16)
        own = blocks[me, span, :]
        for k in range(sup_count):
            part = slice(k * B, (k + 1) * B)
            left = jnp.concatenate([own[:, part]] * 2, axis=0)
            both = jnp.concatenate([high[:, part], low[:, part]], axis=0)
            term = lax.dot_general(
                left, both, (((0,), (0,)), ((), ())), preferred_element_type=jnp.float32
            )
            into[:, :, part] += term.reshape(8, B // 8, B)

    @pl.loop(0, pieces)
    def _(p):
        span = pl.ds(pl.multiple_of(p * PIECE, PIECE), PIECE)
        diag_term(off_ref[span, :], span, partial)

    def to_twin(c):
        return far(partial.at[2 * c + (1 - core)], from_twin.at[c], t_send.at[c], t_recv.at[c], twin, z)

    def to_chip(d):
        return far(
            chip_sum.at[others[d]], from_chips.at[d], c_send.at[d], c_recv.at[d],
            others[d] * 2 + core, z,
        )

    def late_to_twin(c):
        return far(
            late_partial.at[2 * c + (1 - core)], late_twin.at[c], lt_send.at[c], lt_recv.at[c], twin, z
        )

    def late_to_chip(d):
        return far(
            late_code.at[others[d]], code_in.at[d], lc_send.at[d], lc_recv.at[d],
            others[d] * 2 + core, z,
        )

    def late_scale_to_chip(d):
        return far(late_scale, scale_in.at[d], ls_send.at[d], ls_recv.at[d], others[d] * 2 + core, z)

    order = (others[2], others[0], others[1], chip)
    for c in order:
        to_twin(c).start()
    late_partial[...] = jnp.zeros_like(late_partial)
    for d in (2, 0, 1):
        c = others[d]
        to_twin(c).wait_recv()
        chip_sum[c] = partial[2 * c + core] + from_twin[c]
        to_chip(d).start()
    to_twin(chip).wait_recv()
    new_ref[...] = diag_ref[...] + (partial[me] + from_twin[chip])

    @pl.when(z == n - 1)
    def _():
        right_scale(last).wait_recv()

    @pl.when(z == 0)
    def _():
        left_scale(last).wait_recv()

    @pl.when(end)
    def _():
        widen(last)

    @pl.loop(0, pieces)
    def _(p):
        first = pl.multiple_of(p * PIECE, PIECE)
        span = pl.ds(first, PIECE)

        @pl.when(z == n - 1)
        def _():
            right_piece(last, p).wait_recv()

        @pl.when(z == 0)
        def _():
            left_piece(last, p).wait_recv()

        late[...] = jnp.zeros_like(late)

        @pl.when(end)
        def _():
            accumulate(last, first, PIECE, late, pl.ds(0, PIECE))
            diag_term(late[...], span, late_partial)

        off_ref[span, :] = -((off_ref[span, :] + late[...]) * mask)

    @pl.when(end)
    def _():
        for c in order:
            late_to_twin(c).start()
        for d in range(3):
            to_chip(d).wait_recv()
            new_ref[...] += from_chips[d]
        for d in (2, 0, 1):
            c = others[d]
            late_to_twin(c).wait_recv()
            late_sum[c] = late_partial[2 * c + core] + late_twin[c]
        late_to_twin(chip).wait_recv()
        late_sum[chip] = jnp.zeros(late_sum.shape[1:], jnp.float32)
        share = late_sum.shape[1]
        value = late_sum[...].reshape(4 * share, cols)
        top = jnp.max(jnp.abs(value), axis=1, keepdims=True)
        some = top > 1e-33
        held = jnp.where(some, top, 1.0)
        ready = value * jnp.where(some, 32767.0 / held, 0.0)
        ready = ready + jnp.where(ready >= 0.0, 0.5, -0.5)
        late_code[...] = ready.astype(jnp.int32).astype(jnp.int16).reshape(4, share, cols)
        late_scale[...] = jnp.broadcast_to(held * (1.0 / 32767.0), (4 * share, 128)).T[:8]
        for d in (2, 0, 1):
            late_to_chip(d).start()
            late_scale_to_chip(d).start()
        new_ref[...] += late_partial[me] + late_twin[chip]
        for d in (0, 1, 2):
            late_scale_to_chip(d).wait_recv()
            late_to_chip(d).wait_recv()
            late_wide[...] = jnp.concatenate([scale_in[d]] * 16, axis=0).T
            unit = late_wide[pl.ds(pl.multiple_of(chip * share, share), share), :]
            unit = jnp.concatenate([unit] * (cols // 128), axis=1)
            new_ref[...] += code_in[d].astype(jnp.int32).astype(jnp.float32) * unit
        for c in order:
            late_to_twin(c).wait_send()
        for d in range(3):
            late_to_chip(d).wait_send()
            late_scale_to_chip(d).wait_send()

    @pl.when(jnp.logical_not(end))
    def _():
        for d in range(3):
            to_chip(d).wait_recv()
            new_ref[...] += from_chips[d]

    for c in order:
        to_twin(c).wait_send()
    for d in range(3):
        to_chip(d).wait_send()
    for h in range(2):
        panel_pass(h).wait_send()
        for d in range(2):
            panel_to(d, h).wait_send()
        for d in range(4):
            panel_twin(d, h).wait_send()
    for s in range(3):
        @pl.when((z >= s) & (z < n - 1))
        def _():
            right_scale(z - s).wait_send()

            @pl.loop(0, pieces)
            def _(p):
                right_piece(z - s, p).wait_send()

        @pl.when((z + s < n) & (z > 0))
        def _():
            left_scale(z + s).wait_send()

            @pl.loop(0, pieces)
            def _(p):
                left_piece(z + s, p).wait_send()


def fused_body(inverse_blocks, panel, diag_inverse, members, counts):
    rows_dev, cols_dev = panel.shape
    depth = inverse_blocks.shape[1]
    shards = lax.axis_size("col")
    pieces = rows_dev // PIECE
    share = diag_inverse.shape[0]
    vmem = pl.BlockSpec(memory_space=pltpu.VMEM)
    dma = pltpu.SemaphoreType.DMA
    return pl.pallas_call(
        fused_kernel,
        out_shape=(
            jax.ShapeDtypeStruct((rows_dev, cols_dev), jnp.float32),
            jax.ShapeDtypeStruct((share, cols_dev), jnp.float32),
        ),
        in_specs=[pl.BlockSpec(memory_space=pltpu.HBM)] * 5,
        out_specs=(vmem, vmem),
        scratch_shapes=[
            pltpu.VMEM(inverse_blocks.shape, jnp.float32),
            pltpu.VMEM(panel.shape, jnp.bfloat16),
            pltpu.VMEM(diag_inverse.shape, jnp.float32),
            pltpu.SMEM(members.shape, jnp.int32),
            pltpu.SMEM(counts.shape, jnp.int32),
            dma((5,)),
            pltpu.VMEM((shards, rows_dev, depth), jnp.int16),
            pltpu.VMEM((shards, 8, rows_dev), jnp.float32),
            pltpu.VMEM((rows_dev, 128), jnp.float32),
            pltpu.VMEM((8, rows_dev, cols_dev), jnp.bfloat16),
            pltpu.VMEM((2 * rows_dev, depth), jnp.bfloat16),
            pltpu.VMEM((8, share, cols_dev), jnp.float32),
            pltpu.VMEM((4, share, cols_dev), jnp.float32),
            pltpu.VMEM((4, share, cols_dev), jnp.float32),
            pltpu.VMEM((3, share, cols_dev), jnp.float32),
            pltpu.VMEM((PIECE, cols_dev), jnp.float32),
            pltpu.VMEM((8, share, cols_dev), jnp.float32),
            pltpu.VMEM((4, share, cols_dev), jnp.float32),
            pltpu.VMEM((4, share, cols_dev), jnp.float32),
            pltpu.VMEM((4, share, cols_dev), jnp.int16),
            pltpu.VMEM((8, 4 * share), jnp.float32),
            pltpu.VMEM((3, share, cols_dev), jnp.int16),
            pltpu.VMEM((3, 8, 4 * share), jnp.float32),
            pltpu.VMEM((4 * share, 128), jnp.float32),
            dma((shards, pieces)), dma((shards, pieces)), dma((shards, pieces)),
            dma((shards,)), dma((shards,)), dma((shards,)),
            dma((8, 2)), dma((2, 2)), dma((2,)), dma((4, 2)), dma((4,)), dma((4,)), dma((3,)), dma((3,)),
            dma((4,)), dma((4,)), dma((3,)), dma((3,)), dma((3,)), dma((3,)),
        ],
        compiler_params=pltpu.CompilerParams(
            collective_id=0, has_side_effects=True, vmem_limit_bytes=56 * 1024 * 1024
        ),
    )(inverse_blocks, panel, diag_inverse, members, counts)


def body(inverse_blocks, panel, diag_inverse, members, counts):
    rows_dev, cols_dev = panel.shape
    sup_count = cols_dev // B
    depth = inverse_blocks.shape[1]
    ancestor = lax.axis_index("row") * rows_dev // B
    column_mask = column_masks(members, counts, ancestor, lax.axis_index("col") * sup_count, sup_count)
    masked = panel * column_mask.astype(jnp.bfloat16)[None, :]
    coded, scale = quantize(inverse_blocks)
    coded_all = lax.all_gather(coded, "col", axis=0, tiled=False)
    scale_all = lax.all_gather(scale, "col", axis=0, tiled=False)
    masked_all = lax.all_gather(masked, "row", axis=0, tiled=True)
    running = jnp.zeros((rows_dev, cols_dev), jnp.float32)
    for shard in range(coded_all.shape[0]):
        high, low = split_code(coded_all[shard])
        part = masked_all[shard * depth : (shard + 1) * depth]
        term = jnp.dot(high, part, preferred_element_type=jnp.float32) + jnp.dot(
            low, part, preferred_element_type=jnp.float32
        )
        running = running + scale_all[shard] * term
    offdiag = -(running * column_mask[None, :])
    off_high = lax.reduce_precision(offdiag, 8, 7)
    off_low = (offdiag - off_high).astype(jnp.bfloat16).reshape(rows_dev, sup_count, B)
    off_high = off_high.astype(jnp.bfloat16).reshape(rows_dev, sup_count, B)
    masked_blocks = masked.reshape(rows_dev, sup_count, B)
    diag_terms = jnp.einsum(
        "ikc,ikd->ckd", masked_blocks, off_high, preferred_element_type=jnp.float32
    ) + jnp.einsum("ikc,ikd->ckd", masked_blocks, off_low, preferred_element_type=jnp.float32)
    summed = lax.psum_scatter(
        diag_terms.reshape(B, sup_count * B), "row", scatter_dimension=0, tiled=True
    )
    return (offdiag, diag_inverse - summed)


def solution(mesh):
    fits = mesh.shape["row"] == 8 and mesh.shape["col"] == 4
    return jax.shard_map(
        fused_body if fits else body,
        mesh=mesh,
        in_specs=(P("row", "col"), P("row", "col"), P("row", "col"), P(), P()),
        out_specs=(P("row", "col"), P("row", "col")),
        check_vma=False,
    )
```
